32 devices in a mesh: dp: 16 (over z, x, core), rows: 2 (over y).
Axes of the slice: x: 2, y: 2, z: 4, core: 2. Of those that a mesh axis runs over, the one named last changes fastest.
Arguments:
- features: bfloat16 [32, 12, 64, 1024], P('dp', 'rows'), may hold values from -8 to 8
- first_atrous_weight: bfloat16 [3, 3, 1024, 256], P(None, None, 'dp'), may hold values from -0.0625 to 0.0625
- second_atrous_weight: bfloat16 [3, 3, 1024, 256], P(None, None, 'dp'), may hold values from -0.0625 to 0.0625
- third_atrous_weight: bfloat16 [3, 3, 1024, 256], P(None, None, 'dp'), may hold values from -0.0625 to 0.0625
- pointwise_weight: bfloat16 [1024, 256], replicated, may hold values from -0.1875 to 0.1875
- pooling_weight: bfloat16 [1024, 256], replicated, may hold values from -0.1875 to 0.1875
- projection_weight: bfloat16 [1280, 256], replicated, may hold values from -0.15625 to 0.15625
- branch_norm_gain: float32 [4, 256], replicated, may hold values from 0.25 to 1.75
- branch_norm_shift: float32 [4, 256], replicated, may hold values from -3 to 3
- projection_norm_gain: float32 [256], replicated, may hold values from 0.25 to 1.75
- projection_norm_shift: float32 [256], replicated, may hold values from -3 to 3
- ghost_group_index: int32 [32], replicated, may hold values from 0 to 7, as said below
Outputs:
- decoder_in: bfloat16 [32, 12, 64, 256], P(None, 'rows', 'dp')
The draws below stay inside these ranges and needn't reach their ends.
Inputs may be any that keep to these rules, and one draw needn't show every extreme that they name: `ghost_group_index`: each of the 8 group ids names exactly 4 images.
All inputs are finite; a program needn't handle non-finite values.
Results may differ from the reference program's by a relative error of at most 0.0014.
The reference program's roundings to bfloat16 on the way (of `branches`, `pooled`, `pool_act` and `joined`) count: a program that leaves them out, or rounds other values in their place, can miss the bound.
Values may be sent and summed in bfloat16 or wider, within the bound.
No kernel may reach another device: no remote copies, remote signals or barrier semaphores. Data moves between devices by JAX's collectives and lax.ppermute only.
A program may use at most 128 MiB of HBM per device.

```python
import jax
import jax.numpy as jnp
from jax import lax

INPUT_CHANNELS = 1024
OUTPUT_CHANNELS = 256
COLS = 64
DILATION_FIRST = 12
DILATION_SECOND = 24
DILATION_THIRD = 36
IMAGES = 32
MAP_ROWS = 12
GROUPS = 8


def draw_features(key, part):
    first_key = jax.random.fold_in(key, 11)
    second_key = jax.random.fold_in(key, 12)
    base = jax.random.normal(first_key, (IMAGES, MAP_ROWS, COLS, INPUT_CHANNELS), jnp.float32)
    offset = jax.random.normal(second_key, (IMAGES, 1, 1, INPUT_CHANNELS), jnp.float32)
    return jnp.clip(base + offset, -8.0, 8.0).astype(jnp.bfloat16)


def draw_ghost_group_index(key, part):
    order = jax.random.permutation(jax.random.fold_in(key, 21), IMAGES)
    return (order // 4).astype(jnp.int32)


def level_of(own_key, dims, pieces, smallest, top_value):
    level, own = 1.0, jax.random.fold_in(own_key, 6)
    for position, parts in pieces:
        heights = jnp.exp(jax.random.uniform(jax.random.fold_in(own, position), (parts,), jnp.float32, smallest / len(pieces), top_value / len(pieces)))
        level = level * jnp.repeat(heights, dims[position] // parts).reshape([-1 if axis == position else 1 for axis in range(len(dims))])
    return level


def bell_draw(key, shape, spread, most, split=(), kind=jnp.bfloat16):
    level = level_of(key, shape, split, -0.22, 0.18) if split else 1.0
    result = jax.random.normal(key, shape, jnp.float32) * spread * level
    return jnp.minimum(jnp.maximum(result, -most), most).astype(kind)


def setup_inputs(seed: int = 0) -> dict:
    key_of = jax.random.split(jax.random.key(seed), 13)
    return {
        "features": draw_features(jax.random.fold_in(key_of[12], 71), 0),
        "first_atrous_weight": bell_draw(key_of[1], (3, 3, INPUT_CHANNELS, OUTPUT_CHANNELS), (9 * INPUT_CHANNELS) ** -0.5, 0.0625, ((2, 16),)),
        "second_atrous_weight": bell_draw(key_of[2], (3, 3, INPUT_CHANNELS, OUTPUT_CHANNELS), (9 * INPUT_CHANNELS) ** -0.5, 0.0625, ((2, 16),)),
        "third_atrous_weight": bell_draw(key_of[3], (3, 3, INPUT_CHANNELS, OUTPUT_CHANNELS), (9 * INPUT_CHANNELS) ** -0.5, 0.0625, ((2, 16),)),
        "pointwise_weight": bell_draw(key_of[4], (INPUT_CHANNELS, OUTPUT_CHANNELS), INPUT_CHANNELS ** -0.5, 0.1875),
        "pooling_weight": bell_draw(key_of[5], (INPUT_CHANNELS, OUTPUT_CHANNELS), INPUT_CHANNELS ** -0.5, 0.1875),
        "projection_weight": bell_draw(key_of[6], (5 * OUTPUT_CHANNELS, OUTPUT_CHANNELS), (5 * OUTPUT_CHANNELS) ** -0.5, 0.15625),
        "branch_norm_gain": jnp.clip(1.0 + 0.15 * jax.random.normal(key_of[7], (4, OUTPUT_CHANNELS), jnp.float32), 0.25, 1.75),
        "branch_norm_shift": bell_draw(key_of[8], (4, OUTPUT_CHANNELS), 0.5, 3.0, (), jnp.float32),
        "projection_norm_gain": jnp.clip(1.0 + 0.15 * jax.random.normal(key_of[9], (OUTPUT_CHANNELS,), jnp.float32), 0.25, 1.75),
        "projection_norm_shift": bell_draw(key_of[10], (OUTPUT_CHANNELS,), 0.5, 3.0, (), jnp.float32),
        "ghost_group_index": draw_ghost_group_index(jax.random.fold_in(key_of[12], 71), 0),
    }


def atrous_branch(image_slice, kernel_weight, dilation_rate):
    branch_output = lax.conv_general_dilated(image_slice[None], kernel_weight, (1, 1), [(dilation_rate, dilation_rate), (dilation_rate, dilation_rate)], rhs_dilation=(dilation_rate, dilation_rate), dimension_numbers=('NHWC', 'HWIO', 'NHWC'), preferred_element_type=jnp.float32)
    return branch_output[0]

def ghost_norm(pre, onehot, gain, shift):
    count = 4.0 * MAP_ROWS * COLS
    first = lax.optimization_barrier(jnp.sum(pre, axis=(1, 2)))
    second = lax.optimization_barrier(jnp.sum(pre * pre, axis=(1, 2)))
    mean = jnp.dot(onehot.T, first, precision=lax.Precision.HIGHEST) / count
    var = jnp.dot(onehot.T, second, precision=lax.Precision.HIGHEST) / count - mean * mean
    inv = lax.rsqrt(var + 1e-05)
    img_mean = jnp.dot(onehot, mean, precision=lax.Precision.HIGHEST)
    img_inv = jnp.dot(onehot, inv, precision=lax.Precision.HIGHEST)
    scaled = (pre - img_mean[:, None, None, :]) * img_inv[:, None, None, :] * gain + shift
    return jax.nn.relu(scaled).astype(jnp.bfloat16)

def reference(features, first_atrous_weight, second_atrous_weight, third_atrous_weight, pointwise_weight, pooling_weight, projection_weight, branch_norm_gain, branch_norm_shift, projection_norm_gain, projection_norm_shift, ghost_group_index):
    onehot = (ghost_group_index[:, None] == jnp.arange(GROUPS, dtype=jnp.int32)[None, :]).astype(jnp.float32)

    def per_image(image_slice):
        pointwise_output = jnp.einsum('hwc,co->hwo', image_slice, pointwise_weight, preferred_element_type=jnp.float32)
        return jnp.concatenate([pointwise_output, atrous_branch(image_slice, first_atrous_weight, DILATION_FIRST), atrous_branch(image_slice, second_atrous_weight, DILATION_SECOND), atrous_branch(image_slice, third_atrous_weight, DILATION_THIRD)], -1)
    pre = lax.map(per_image, features)
    branches = ghost_norm(pre, onehot, branch_norm_gain.reshape(-1), branch_norm_shift.reshape(-1))
    pooled = (lax.optimization_barrier(jnp.sum(features, axis=(1, 2), dtype=jnp.float32)) / (MAP_ROWS * COLS)).astype(jnp.bfloat16)
    pool_act = jax.nn.relu(jnp.dot(pooled, pooling_weight, preferred_element_type=jnp.float32)).astype(jnp.bfloat16)
    pool_map = jnp.broadcast_to(pool_act[:, None, None, :], (IMAGES, MAP_ROWS, COLS, OUTPUT_CHANNELS))
    joined = jnp.concatenate([branches, pool_map], -1)
    proj = jnp.einsum('nhwc,co->nhwo', joined, projection_weight, preferred_element_type=jnp.float32)
    return ghost_norm(proj, onehot, projection_norm_gain, projection_norm_shift)
```

```python
import functools

import jax
import jax.numpy as jnp
from jax import lax
from jax.experimental import pallas as pl
from jax.experimental.pallas import tpu as pltpu
from jax.sharding import PartitionSpec as P

DILATIONS = (12, 24, 36)
VMEM = pltpu.VMEM
SMEM = pltpu.SMEM


def from_behind(array, axis, by):
    count = lax.axis_size(axis)
    pairs = [(i, i + by) for i in range(count) if 0 <= i + by < count]
    return lax.ppermute(array, axis, pairs)


def swap(array, axis, mask):
    return lax.ppermute(array, axis, [(i, i ^ mask) for i in range(lax.axis_size(axis))])


def masks_of(axis):
    size, mask, out = lax.axis_size(axis), 1, []
    while mask < size:
        out.append(mask)
        mask *= 2
    return out


def sum_over(array, axes):
    for axis in axes:
        size = lax.axis_size(axis)
        if size & (size - 1):
            array = lax.psum(array, axis)
            continue
        for mask in masks_of(axis):
            array = array + swap(array, axis, mask)
    return array


def tap_span(cols, shift):
    low = max(0, -shift) // 16 * 16
    high = min(cols, -(-(cols - max(0, shift)) // 16) * 16)
    return low, high


def moved(part, low, cols, shift):
    rows, wide, chans = part.shape
    if shift > 0:
        zeros = jnp.zeros((rows, shift, chans), part.dtype)
        return jnp.concatenate([zeros, part[:, : cols - shift]], axis=1)
    zeros = jnp.zeros((rows, -shift, chans), part.dtype)
    return jnp.concatenate([part[:, -shift - low :], zeros], axis=1)


def group_rows(groups, group, values):
    rows = lax.broadcasted_iota(jnp.int32, (groups, values.shape[-1]), 0)
    return jnp.where(rows == group, jnp.broadcast_to(values, rows.shape), 0.0)


def pick_row(table, group):
    rows = lax.broadcasted_iota(jnp.int32, table.shape, 0)
    return jnp.sum(jnp.where(rows == group, table, 0.0), axis=0, keepdims=True)


def conv_kernel(groups, n_blocks, owners, gids, x_ref, *rest):
    pieces, (pw_ref, pre_ref, stats_ref, w_ref) = rest[:n_blocks], rest[n_blocks:]
    images, rows, cols, chans = x_ref.shape
    outs = pw_ref.shape[1]
    depth = pieces[0].shape[2]
    at = 0
    for block in pieces:
        for j in range(block.shape[0]):
            start = pl.multiple_of(owners[at] * depth, depth)
            w_ref[:, pl.ds(start, depth), :] = block[j]
            at += 1
    stats_ref[...] = jnp.zeros_like(stats_ref)

    def product(x, w):
        r, c, _ = x.shape
        y = jnp.dot(x.reshape(r * c, chans), w, preferred_element_type=jnp.float32)
        return y.reshape(r, c, outs)

    def image(i, carry):
        group = gids[i]

        def emit(branch, value):
            span = pl.ds(branch * outs, outs)
            pre_ref[i, :, :, span] = value
            first = jnp.sum(value, axis=(0, 1)).reshape(1, outs)
            second = jnp.sum(value * value, axis=(0, 1)).reshape(1, outs)
            stats_ref[pl.ds(0, groups), span] += group_rows(groups, group, first)
            stats_ref[pl.ds(groups, groups), span] += group_rows(groups, group, second)

        emit(0, product(x_ref[i], pw_ref[...]))
        for k, dilation in enumerate(DILATIONS):
            total = product(x_ref[i], w_ref[3 * k + 1])
            for tap, shift in ((0, dilation), (2, -dilation)):
                if abs(shift) < cols:
                    low, high = tap_span(cols, shift)
                    part = product(x_ref[i, :, pl.ds(low, high - low), :], w_ref[3 * k + tap])
                    total = total + moved(part, low, cols, shift)
            emit(k + 1, total)
        return carry

    lax.fori_loop(0, images, image, 0)


def conv_and_stats(features, pieces, owners, own_groups, pointwise_weight, groups):
    images, rows, cols, chans = features.shape
    taps = pieces[0].shape[1]
    outs = pointwise_weight.shape[1]
    width = outs * (1 + len(DILATIONS))
    return pl.pallas_call(
        functools.partial(conv_kernel, groups, len(pieces)),
        out_shape=(
            jax.ShapeDtypeStruct((images, rows, cols, width), jnp.float32),
            jax.ShapeDtypeStruct((2 * groups, width), jnp.float32),
        ),
        in_specs=[pl.BlockSpec(memory_space=SMEM)] * 2
        + [pl.BlockSpec(memory_space=VMEM)] * (2 + len(pieces)),
        out_specs=(pl.BlockSpec(memory_space=VMEM),) * 2,
        scratch_shapes=[pltpu.VMEM((taps, chans, outs), pointwise_weight.dtype)],
        name="conv",
    )(owners, own_groups, features, *pieces, pointwise_weight)


def project_kernel(groups, count, gids, pre_ref, total_ref, gain_ref, shift_ref, w_ref, pool_ref, proj_ref, stats_ref):
    images, rows, cols, width = pre_ref.shape
    outs = w_ref.shape[1]
    stats_ref[...] = jnp.zeros_like(stats_ref)

    def image(i, carry):
        group = gids[i]
        mean = pick_row(total_ref[pl.ds(0, groups), :], group) / count
        var = pick_row(total_ref[pl.ds(groups, groups), :], group) / count - mean * mean
        inv = lax.rsqrt(var + 1e-05)
        pre = pre_ref[i].reshape(rows * cols, width)
        scaled = (pre - mean) * inv * gain_ref[...] + shift_ref[...]
        branches = jnp.maximum(scaled, 0.0).astype(w_ref.dtype)
        proj = jnp.dot(branches, w_ref[...], preferred_element_type=jnp.float32)
        proj = proj + pool_ref[pl.ds(i, 1), :]
        proj_ref[i] = proj.reshape(rows, cols, outs)
        first = jnp.sum(proj, axis=0, keepdims=True)
        second = jnp.sum(proj * proj, axis=0, keepdims=True)
        stats_ref[pl.ds(0, groups), :] += group_rows(groups, group, first)
        stats_ref[pl.ds(groups, groups), :] += group_rows(groups, group, second)
        return carry

    lax.fori_loop(0, images, image, 0)


def normed_project(pre, totals, own_groups, gain, shift, weight, pool_term, groups, count):
    images, rows, cols, _ = pre.shape
    outs = weight.shape[1]
    return pl.pallas_call(
        functools.partial(project_kernel, groups, count),
        out_shape=(
            jax.ShapeDtypeStruct((images, rows, cols, outs), jnp.float32),
            jax.ShapeDtypeStruct((2 * groups, outs), jnp.float32),
        ),
        in_specs=[pl.BlockSpec(memory_space=SMEM)] + [pl.BlockSpec(memory_space=VMEM)] * 6,
        out_specs=(pl.BlockSpec(memory_space=VMEM),) * 2,
        name="project",
    )(own_groups, pre, totals, gain, shift, weight, pool_term)


def gathered_pieces(own):
    size = lax.axis_size("dp")
    me = lax.axis_index("dp")
    quarter = size // 4
    far = [quarter * j for j in range(1, 4)]
    near = list(range(2, quarter, 2))
    line = {0: own}
    for mask in far:
        line[mask] = swap(own, "dp", mask)
    relayed = {}
    for mask in line:
        for other in near:
            relayed[mask ^ other] = swap(line[mask], "dp", other)
    early = [m for m in line] + [m for m in near]
    late = [m for m in relayed if m not in near]
    everything = {**line, **relayed}
    pieces, order = [], []
    for masks in (early, late):
        stack = jnp.stack([everything[m] for m in masks])
        pieces += [stack, swap(stack, "dp", 1)]
        order += [m for m in masks] + [m ^ 1 for m in masks]
    owners = jnp.stack([me ^ m for m in order]).astype(jnp.int32)
    return pieces, owners


def row_tap_list(block_tensor, kernel_row_slice, dilation_rate):
    partial_terms = jnp.einsum(
        "irwc,kco->irwko", block_tensor, kernel_row_slice, preferred_element_type=jnp.float32
    )
    map_width = block_tensor.shape[2]
    left = jnp.pad(partial_terms[:, :, :, 0], ((0, 0), (0, 0), (dilation_rate, 0), (0, 0)))
    right = jnp.pad(partial_terms[:, :, :, 2], ((0, 0), (0, 0), (0, dilation_rate), (0, 0)))
    return partial_terms[:, :, :, 1] + left[:, :, :map_width] + right[:, :, dilation_rate:]


def general_pre(features, kernels, pointwise_weight):
    branches = [
        jnp.einsum("irwc,co->irwo", features, pointwise_weight, preferred_element_type=jnp.float32)
    ]
    for kernel, dilation in zip(kernels, DILATIONS):
        whole = lax.all_gather(kernel, "dp", axis=2, tiled=True)
        total = row_tap_list(features, whole[1], dilation)
        step = dilation // features.shape[1]
        if step < lax.axis_size("rows"):
            for by, tap in ((step, 0), (-step, 2)):
                total = total + from_behind(row_tap_list(features, whole[tap], dilation), "rows", by)
        branches.append(total)
    return jnp.concatenate(branches, -1)


def shards(
    features,
    first_atrous_weight,
    second_atrous_weight,
    third_atrous_weight,
    pointwise_weight,
    pooling_weight,
    projection_weight,
    branch_norm_gain,
    branch_norm_shift,
    projection_norm_gain,
    projection_norm_shift,
    ghost_group_index,
):
    images, rows_dev, cols, chans = features.shape
    dp_size = lax.axis_size("dp")
    rows_size = lax.axis_size("rows")
    groups = images * dp_size // 4
    pixels = rows_dev * rows_size * cols
    count = 4.0 * pixels
    width = branch_norm_gain.size
    own_groups = lax.dynamic_slice_in_dim(
        ghost_group_index, lax.axis_index("dp") * images, images, 0
    )
    kernels = (first_atrous_weight, second_atrous_weight, third_atrous_weight)
    middle_only = all(d // rows_dev >= rows_size for d in DILATIONS)
    if middle_only and dp_size >= 8 and dp_size & (dp_size - 1) == 0:
        own = jnp.concatenate([kernel[1] for kernel in kernels], 0)
        pieces, owners = gathered_pieces(own)
        pre, stats = conv_and_stats(
            features, pieces, owners, own_groups, pointwise_weight, groups
        )
    else:
        pre = general_pre(features, kernels, pointwise_weight)
        hot = (own_groups[:, None] == jnp.arange(groups, dtype=jnp.int32)[None, :]).astype(jnp.float32)
        stats = jnp.concatenate(
            [
                jnp.dot(hot.T, jnp.sum(t, axis=(1, 2)), precision=lax.Precision.HIGHEST)
                for t in (pre, pre * pre)
            ],
            0,
        )
    pool_total = sum_over(jnp.sum(features, axis=(1, 2), dtype=jnp.float32), ("rows",))
    pooled = (pool_total / pixels).astype(jnp.bfloat16)
    pool_act = jax.nn.relu(
        jnp.dot(pooled, pooling_weight, preferred_element_type=jnp.float32)
    ).astype(jnp.bfloat16)
    pool_term = jnp.dot(pool_act, projection_weight[width:], preferred_element_type=jnp.float32)
    totals = sum_over(stats, ("dp", "rows"))
    proj, proj_stats = normed_project(
        pre,
        totals,
        own_groups,
        branch_norm_gain.reshape(1, -1),
        branch_norm_shift.reshape(1, -1),
        projection_weight[:width],
        pool_term,
        groups,
        count,
    )
    proj_totals = sum_over(proj_stats, ("dp", "rows"))
    hot = own_groups[:, None] == jnp.arange(groups, dtype=jnp.int32)[None, :]
    own_totals = jnp.sum(
        jnp.where(hot[None, :, :, None], proj_totals.reshape(2, 1, groups, -1), 0.0), axis=2
    )
    mean = own_totals[0] / count
    var = own_totals[1] / count - mean * mean
    inv = lax.rsqrt(var + 1e-05)
    scaled = (proj - mean[:, None, None, :]) * inv[:, None, None, :]
    scaled = scaled * projection_norm_gain + projection_norm_shift
    local_out = jax.nn.relu(scaled).astype(jnp.bfloat16)
    return lax.all_to_all(local_out, "dp", split_axis=2, concat_axis=0, tiled=True)


def solution(mesh):
    in_specs = (
        P("dp", "rows", None, None),
        P(None, None, "dp", None),
        P(None, None, "dp", None),
        P(None, None, "dp", None),
        P(),
        P(),
        P(),
        P(),
        P(),
        P(),
        P(),
        P(),
    )
    out_specs = P(None, "rows", "dp", None)
    return jax.shard_map(shards, mesh=mesh, in_specs=in_specs, out_specs=out_specs, check_vma=False)
```

```python
import functools

import jax
import jax.numpy as jnp
from jax import lax
from jax.experimental import pallas as pl
from jax.experimental.pallas import tpu as pltpu
from jax.sharding import PartitionSpec as P

DILATIONS = (12, 24, 36)
VMEM = pltpu.VMEM
SMEM = pltpu.SMEM
VMEM_LIMIT = 26 * 2**20


def from_behind(array, axis, by):
    count = lax.axis_size(axis)
    pairs = [(i, i + by) for i in range(count) if 0 <= i + by < count]
    return lax.ppermute(array, axis, pairs)


def swap(array, axis, mask):
    return lax.ppermute(array, axis, [(i, i ^ mask) for i in range(lax.axis_size(axis))])


def masks_of(axis):
    size, mask, out = lax.axis_size(axis), 1, []
    while mask < size:
        out.append(mask)
        mask *= 2
    return out


def sum_over(array, axes):
    for axis in axes:
        size = lax.axis_size(axis)
        if size & (size - 1):
            array = lax.psum(array, axis)
            continue
        for mask in masks_of(axis):
            array = array + swap(array, axis, mask)
    return array


def tap_span(cols, shift):
    low = max(0, -shift) // 16 * 16
    high = min(cols, -(-(cols - max(0, shift)) // 16) * 16)
    return low, high


def moved(part, low, cols, shift):
    rows, _, chans = part.shape
    if shift > 0:
        zeros = jnp.zeros((rows, shift, chans), part.dtype)
        return jnp.concatenate([zeros, part[:, : cols - shift]], axis=1)
    zeros = jnp.zeros((rows, -shift, chans), part.dtype)
    return jnp.concatenate([part[:, -shift - low :], zeros], axis=1)


def group_rows(groups, group, values):
    rows = lax.broadcasted_iota(jnp.int32, (groups, values.shape[-1]), 0)
    return jnp.where(rows == group, jnp.broadcast_to(values, rows.shape), 0.0)


def pick_row(table, group):
    rows = lax.broadcasted_iota(jnp.int32, table.shape, 0)
    return jnp.sum(jnp.where(rows == group, table, 0.0), axis=0, keepdims=True)


def conv_kernel(groups, masks, opens, closes, index_ref, x_ref, own_ref, other_ref, *rest):
    if opens:
        pw_ref, pre_ref, *rest = rest
    else:
        done_ref, pre_ref, *rest = rest
    if closes:
        stats_ref, *rest = rest
        stats_ref[...] = jnp.zeros_like(stats_ref)
    w_ref, part_ref = rest
    images, _, cols, _ = x_ref.shape
    outs = w_ref.shape[2]
    depth = own_ref.shape[2]
    pair = 2 * depth
    me = lax.axis_index("dp")
    odd = lax.rem(lax.axis_index("rows"), 2)
    core = lax.rem(me, 2)
    here = pl.multiple_of(core * depth, depth)
    there = pl.multiple_of((1 - core) * depth, depth)
    for j, mask in enumerate(masks):
        w_ref[:, pl.ds(j * pair + here, depth), :] = own_ref[j]
        w_ref[:, pl.ds(j * pair + there, depth), :] = other_ref[j]
        mask = mask[0] + odd * (mask[1] - mask[0])
        block = pl.multiple_of((me ^ mask) // 2 * pair, pair)
        part_ref[:, :, :, pl.ds(j * pair, pair)] = x_ref[:, :, :, pl.ds(block, pair)]

    def product(x, w):
        r, c, k = x.shape
        y = jnp.dot(x.reshape(r * c, k), w, preferred_element_type=jnp.float32)
        return y.reshape(r, c, outs)

    def image(i, carry):
        group = index_ref[me * images + i]

        def emit(branch, value):
            span = pl.ds(branch * outs, outs)
            if branch == 0 and not opens:
                value = done_ref[i, :, :, span]
            elif not opens:
                value = value + done_ref[i, :, :, span]
            pre_ref[i, :, :, span] = value
            if closes:
                first = jnp.sum(value, axis=(0, 1)).reshape(1, outs)
                second = jnp.sum(value * value, axis=(0, 1)).reshape(1, outs)
                stats_ref[pl.ds(0, groups), span] += group_rows(groups, group, first)
                stats_ref[pl.ds(groups, groups), span] += group_rows(groups, group, second)

        if opens:
            emit(0, product(x_ref[i], pw_ref[...]))
        elif closes:
            emit(0, None)
        for k, dilation in enumerate(DILATIONS):
            total = product(part_ref[i], w_ref[3 * k + 1])
            for tap, shift in ((0, dilation), (2, -dilation)):
                if abs(shift) < cols:
                    low, high = tap_span(cols, shift)
                    part = product(part_ref[i, :, pl.ds(low, high - low), :], w_ref[3 * k + tap])
                    total = total + moved(part, low, cols, shift)
            emit(k + 1, total)
        return carry

    lax.fori_loop(0, images, image, 0)


def conv_part(features, stack, index, groups, opening=None, done=None, closes=False):
    masks, own, other = stack
    images, rows, cols, _ = features.shape
    _, taps, depth, outs = own.shape
    share = 2 * depth * len(masks)
    width = outs * (1 + len(DILATIONS))
    pre = jax.ShapeDtypeStruct((images, rows, cols, width), jnp.float32)
    stats = jax.ShapeDtypeStruct((2 * groups, width), jnp.float32)
    opens = done is None
    return pl.pallas_call(
        functools.partial(conv_kernel, groups, masks, opens, closes),
        out_shape=(pre, stats) if closes else (pre,),
        in_specs=[pl.BlockSpec(memory_space=SMEM)] + [pl.BlockSpec(memory_space=VMEM)] * 4,
        out_specs=(pl.BlockSpec(memory_space=VMEM),) * (2 if closes else 1),
        scratch_shapes=[
            pltpu.VMEM((taps, share, outs), own.dtype),
            pltpu.VMEM((images, rows, cols, share), features.dtype),
        ],
        input_output_aliases={} if opens else {4: 0},
        compiler_params=pltpu.CompilerParams(vmem_limit_bytes=VMEM_LIMIT),
    )(index, features, own, other, opening if opens else done)


def pick_kernel(*refs):
    *ins, out, sems = refs
    at, copies = 0, []
    for j, ref in enumerate(ins):
        copy = pltpu.make_async_copy(ref.at[1], out.at[pl.ds(at, ref.shape[1])], sems.at[j])
        copy.start()
        copies.append(copy)
        at += ref.shape[1]
    for copy in copies:
        copy.wait()


def middle_rows(kernels):
    _, taps, depth, outs = kernels[0].shape
    return pl.pallas_call(
        pick_kernel,
        out_shape=jax.ShapeDtypeStruct((taps * len(kernels), depth, outs), kernels[0].dtype),
        in_specs=[pl.BlockSpec(memory_space=pltpu.HBM)] * len(kernels),
        out_specs=pl.BlockSpec(memory_space=VMEM),
        scratch_shapes=[pltpu.SemaphoreType.DMA((len(kernels),))],
        compiler_params=pltpu.CompilerParams(vmem_limit_bytes=VMEM_LIMIT // 4),
        name="pick",
    )(*[pltpu.with_memory_space_constraint(kernel, pltpu.HBM) for kernel in kernels])


def project_kernel(groups, count, index_ref, pre_ref, total_ref, gain_ref, shift_ref, w_ref, pool_ref, proj_ref, stats_ref):
    images, rows, cols, width = pre_ref.shape
    outs = w_ref.shape[1]
    me = lax.axis_index("dp")
    stats_ref[...] = jnp.zeros_like(stats_ref)
    gain = jnp.concatenate([gain_ref[pl.ds(k, 1), :] for k in range(gain_ref.shape[0])], 1)
    shift = jnp.concatenate([shift_ref[pl.ds(k, 1), :] for k in range(shift_ref.shape[0])], 1)

    def image(i, carry):
        group = index_ref[me * images + i]
        mean = pick_row(total_ref[pl.ds(0, groups), :], group) / count
        var = pick_row(total_ref[pl.ds(groups, groups), :], group) / count - mean * mean
        inv = lax.rsqrt(var + 1e-05)
        pre = pre_ref[i].reshape(rows * cols, width)
        scaled = (pre - mean) * inv * gain + shift
        branches = jnp.maximum(scaled, 0.0).astype(w_ref.dtype)
        proj = jnp.dot(branches, w_ref[pl.ds(0, width), :], preferred_element_type=jnp.float32)
        proj = proj + pool_ref[pl.ds(i, 1), :]
        proj_ref[i] = proj.reshape(rows, cols, outs)
        first = jnp.sum(proj, axis=0, keepdims=True)
        second = jnp.sum(proj * proj, axis=0, keepdims=True)
        stats_ref[pl.ds(0, groups), :] += group_rows(groups, group, first)
        stats_ref[pl.ds(groups, groups), :] += group_rows(groups, group, second)
        return carry

    lax.fori_loop(0, images, image, 0)


def normed_project(pre, totals, index, gain, shift, weight, pool_term, groups, count):
    images, rows, cols, _ = pre.shape
    outs = weight.shape[1]
    return pl.pallas_call(
        functools.partial(project_kernel, groups, count),
        out_shape=(
            jax.ShapeDtypeStruct((images, rows, cols, outs), jnp.float32),
            jax.ShapeDtypeStruct((2 * groups, outs), jnp.float32),
        ),
        in_specs=[pl.BlockSpec(memory_space=SMEM)] + [pl.BlockSpec(memory_space=VMEM)] * 6,
        out_specs=(pl.BlockSpec(memory_space=VMEM),) * 2,
        compiler_params=pltpu.CompilerParams(vmem_limit_bytes=VMEM_LIMIT),
        name="project",
    )(index, pre, totals, gain, shift, weight, pool_term)


def both_cores(got, masks):
    stack = jnp.stack([got[m] for m in masks])
    return tuple(masks), stack, swap(stack, "dp", 1)


def far_swap(array, even, odd):
    count = lax.axis_size("rows")
    pairs = []
    for i in range(lax.axis_size("dp")):
        for j in range(count):
            k = i ^ (odd if j % 2 else even)
            pairs.append((i * count + j, k * count + j))
    return lax.ppermute(array, ("dp", "rows"), pairs)


def conv_branches(features, kernels, pointwise_weight, pool_term, index, groups):
    quarter = lax.axis_size("dp") // 4
    near = list(range(2, quarter, 2))
    one, two, three = quarter, 2 * quarter, 3 * quarter
    own = middle_rows(kernels)
    both, first, second = (one, one), (two, three), (three, two)

    def by(share, mask):
        return tuple(m ^ mask for m in share)

    got = {(0, 0): own}
    got[first] = far_swap(own, *first)
    got[both] = swap(own, "dp", one)
    for mask in near:
        got[(mask, mask)] = swap(own, "dp", mask)
    for mask in near:
        got[by(first, mask)] = swap(got[first], "dp", mask)
    got[second] = swap(got[first], "rows", 1)
    for mask in near:
        got[by(both, mask)] = swap(got[both], "dp", mask)
    masks, *stack = both_cores(got, [(0, 0), both] + [(m, m) for m in near])
    stack, pool_term = lax.optimization_barrier((stack, pool_term))
    (done,) = conv_part(features, (masks, *stack), index, groups, pointwise_weight)
    for mask in near:
        late = by(first, mask)
        got[late], done = lax.optimization_barrier((got[late], done))
        got[by(second, mask)] = swap(got[late], "rows", 1)
    middle = [first, second] + [by(both, m) for m in near] + [by(first, m) for m in near]
    last = [by(second, m) for m in near]
    (done,) = conv_part(features, both_cores(got, middle), index, groups, done=done)
    pre, stats = conv_part(features, both_cores(got, last), index, groups, done=done, closes=True)
    return pre, stats, pool_term


def row_tap_list(block_tensor, kernel_row_slice, dilation_rate):
    partial_terms = jnp.einsum(
        "irwc,kco->irwko", block_tensor, kernel_row_slice, preferred_element_type=jnp.float32
    )
    map_width = block_tensor.shape[2]
    left = jnp.pad(partial_terms[:, :, :, 0], ((0, 0), (0, 0), (dilation_rate, 0), (0, 0)))
    right = jnp.pad(partial_terms[:, :, :, 2], ((0, 0), (0, 0), (0, dilation_rate), (0, 0)))
    return partial_terms[:, :, :, 1] + left[:, :, :map_width] + right[:, :, dilation_rate:]


def general_pre(features, kernels, pointwise_weight):
    branches = [
        jnp.einsum("irwc,co->irwo", features, pointwise_weight, preferred_element_type=jnp.float32)
    ]
    for kernel, dilation in zip(kernels, DILATIONS):
        whole = lax.all_gather(kernel, "dp", axis=2, tiled=True)
        total = row_tap_list(features, whole[1], dilation)
        step = dilation // features.shape[1]
        if step < lax.axis_size("rows"):
            for by, tap in ((step, 0), (-step, 2)):
                total = total + from_behind(row_tap_list(features, whole[tap], dilation), "rows", by)
        branches.append(total)
    return jnp.concatenate(branches, -1)


def shards(
    features,
    first_atrous_weight,
    second_atrous_weight,
    third_atrous_weight,
    pointwise_weight,
    pooling_weight,
    projection_weight,
    branch_norm_gain,
    branch_norm_shift,
    projection_norm_gain,
    projection_norm_shift,
    ghost_group_index,
):
    images, rows_dev, cols, _ = features.shape
    dp_size = lax.axis_size("dp")
    rows_size = lax.axis_size("rows")
    groups = images * dp_size // 4
    pixels = rows_dev * rows_size * cols
    count = 4.0 * pixels
    width = branch_norm_gain.size
    own_groups = lax.dynamic_slice_in_dim(
        ghost_group_index, lax.axis_index("dp") * images, images, 0
    )
    kernels = (first_atrous_weight, second_atrous_weight, third_atrous_weight)
    pool_total = sum_over(jnp.sum(features, axis=(1, 2), dtype=jnp.float32), ("rows",))
    pooled = (pool_total / pixels).astype(jnp.bfloat16)
    pool_act = jax.nn.relu(
        jnp.dot(pooled, pooling_weight, preferred_element_type=jnp.float32)
    ).astype(jnp.bfloat16)
    pool_term = jnp.dot(pool_act, projection_weight[width:], preferred_element_type=jnp.float32)
    middle_only = all(d // rows_dev >= rows_size for d in DILATIONS)
    if middle_only and rows_size % 2 == 0 and dp_size >= 8 and dp_size & (dp_size - 1) == 0:
        pre, stats, pool_term = conv_branches(
            features, kernels, pointwise_weight, pool_term, ghost_group_index, groups
        )
    else:
        pre = general_pre(features, kernels, pointwise_weight)
        hot = (own_groups[:, None] == jnp.arange(groups, dtype=jnp.int32)[None, :]).astype(jnp.float32)
        stats = jnp.concatenate(
            [
                jnp.dot(hot.T, jnp.sum(t, axis=(1, 2)), precision=lax.Precision.HIGHEST)
                for t in (pre, pre * pre)
            ],
            0,
        )
    totals = sum_over(stats, ("dp", "rows"))
    proj, proj_stats = normed_project(
        pre,
        totals,
        ghost_group_index,
        branch_norm_gain,
        branch_norm_shift,
        projection_weight,
        pool_term,
        groups,
        count,
    )
    proj_totals = sum_over(proj_stats, ("dp", "rows"))
    hot = own_groups[:, None] == jnp.arange(groups, dtype=jnp.int32)[None, :]
    own_totals = jnp.sum(
        jnp.where(hot[None, :, :, None], proj_totals.reshape(2, 1, groups, -1), 0.0), axis=2
    )
    mean = own_totals[0] / count
    var = own_totals[1] / count - mean * mean
    inv = lax.rsqrt(var + 1e-05)
    scaled = (proj - mean[:, None, None, :]) * inv[:, None, None, :]
    scaled = scaled * projection_norm_gain + projection_norm_shift
    local_out = jax.nn.relu(scaled).astype(jnp.bfloat16)
    return lax.all_to_all(local_out, "dp", split_axis=2, concat_axis=0, tiled=True)


def solution(mesh):
    in_specs = (
        P("dp", "rows", None, None),
        P(None, None, "dp", None),
        P(None, None, "dp", None),
        P(None, None, "dp", None),
        P(),
        P(),
        P(),
        P(),
        P(),
        P(),
        P(),
        P(),
    )
    out_specs = P(None, "rows", "dp", None)

    return jax.shard_map(shards, mesh=mesh, in_specs=in_specs, out_specs=out_specs, check_vma=False)
```

```python
import functools

import jax
import jax.numpy as jnp
from jax import lax
from jax.experimental import pallas as pl
from jax.experimental.pallas import tpu as pltpu
from jax.sharding import PartitionSpec as P

DILATIONS = (12, 24, 36)
VMEM = pltpu.VMEM
SMEM = pltpu.SMEM
VMEM_LIMIT = 26 * 2**20


def from_behind(array, axis, by):
    count = lax.axis_size(axis)
    pairs = [(i, i + by) for i in range(count) if 0 <= i + by < count]
    return lax.ppermute(array, axis, pairs)


def swap(array, axis, mask):
    return lax.ppermute(array, axis, [(i, i ^ mask) for i in range(lax.axis_size(axis))])


def masks_of(axis):
    size, mask, out = lax.axis_size(axis), 1, []
    while mask < size:
        out.append(mask)
        mask *= 2
    return out


def sum_over(array, axes):
    for axis in axes:
        size = lax.axis_size(axis)
        if size & (size - 1):
            array = lax.psum(array, axis)
            continue
        for mask in masks_of(axis):
            array = array + swap(array, axis, mask)
    return array


def tap_span(cols, shift):
    low = max(0, -shift) // 16 * 16
    high = min(cols, -(-(cols - max(0, shift)) // 16) * 16)
    return low, high


def moved(part, low, cols, shift):
    rows, _, chans = part.shape
    if shift > 0:
        zeros = jnp.zeros((rows, shift, chans), part.dtype)
        return jnp.concatenate([zeros, part[:, : cols - shift]], axis=1)
    zeros = jnp.zeros((rows, -shift, chans), part.dtype)
    return jnp.concatenate([part[:, -shift - low :], zeros], axis=1)


def group_rows(groups, group, values):
    rows = lax.broadcasted_iota(jnp.int32, (groups, values.shape[-1]), 0)
    return jnp.where(rows == group, jnp.broadcast_to(values, rows.shape), 0.0)


def pick_row(table, group):
    rows = lax.broadcasted_iota(jnp.int32, table.shape, 0)
    return jnp.sum(jnp.where(rows == group, table, 0.0), axis=0, keepdims=True)


def conv_kernel(groups, masks, opens, closes, index_ref, x_ref, *rest):
    shares, rest = rest[: 2 * len(masks)], rest[2 * len(masks) :]
    if opens:
        pw_ref, pre_ref, *rest = rest
    else:
        done_ref, pre_ref, *rest = rest
    if closes:
        stats_ref, *rest = rest
        stats_ref[...] = jnp.zeros_like(stats_ref)
    w_ref, part_ref = rest
    images, _, cols, _ = x_ref.shape
    outs = w_ref.shape[2]
    depth = shares[0].shape[1]
    pair = 2 * depth
    me = lax.axis_index("dp")
    odd = lax.rem(lax.axis_index("rows"), 2)
    core = lax.rem(me, 2)
    here = pl.multiple_of(core * depth, depth)
    there = pl.multiple_of((1 - core) * depth, depth)
    for j, mask in enumerate(masks):
        w_ref[:, pl.ds(j * pair + here, depth), :] = shares[2 * j][...]
        w_ref[:, pl.ds(j * pair + there, depth), :] = shares[2 * j + 1][...]
        mask = mask[0] + odd * (mask[1] - mask[0])
        block = pl.multiple_of((me ^ mask) // 2 * pair, pair)
        part_ref[:, :, :, pl.ds(j * pair, pair)] = x_ref[:, :, :, pl.ds(block, pair)]

    def product(x, w):
        r, c, k = x.shape
        y = jnp.dot(x.reshape(r * c, k), w, preferred_element_type=jnp.float32)
        return y.reshape(r, c, outs)

    def image(i, carry):
        group = index_ref[me * images + i]

        def emit(branch, value):
            span = pl.ds(branch * outs, outs)
            if branch == 0 and not opens:
                value = done_ref[i, :, :, span]
            elif not opens:
                value = value + done_ref[i, :, :, span]
            pre_ref[i, :, :, span] = value
            if closes:
                first = jnp.sum(value, axis=(0, 1)).reshape(1, outs)
                second = jnp.sum(value * value, axis=(0, 1)).reshape(1, outs)
                stats_ref[pl.ds(0, groups), span] += group_rows(groups, group, first)
                stats_ref[pl.ds(groups, groups), span] += group_rows(groups, group, second)

        if opens:
            emit(0, product(x_ref[i], pw_ref[...]))
        elif closes:
            emit(0, None)
        for k, dilation in enumerate(DILATIONS):
            total = product(part_ref[i], w_ref[3 * k + 1])
            for tap, shift in ((0, dilation), (2, -dilation)):
                if abs(shift) < cols:
                    low, high = tap_span(cols, shift)
                    part = product(part_ref[i, :, pl.ds(low, high - low), :], w_ref[3 * k + tap])
                    total = total + moved(part, low, cols, shift)
            emit(k + 1, total)
        return carry

    lax.fori_loop(0, images, image, 0)


def conv_part(features, held, masks, index, groups, opening=None, done=None, closes=False):
    shares = [share for mask in masks for share in held[mask]]
    images, rows, cols, _ = features.shape
    taps, depth, outs = shares[0].shape
    share = 2 * depth * len(masks)
    width = outs * (1 + len(DILATIONS))
    pre = jax.ShapeDtypeStruct((images, rows, cols, width), jnp.float32)
    stats = jax.ShapeDtypeStruct((2 * groups, width), jnp.float32)
    opens = done is None
    return pl.pallas_call(
        functools.partial(conv_kernel, groups, tuple(masks), opens, closes),
        out_shape=(pre, stats) if closes else (pre,),
        in_specs=[pl.BlockSpec(memory_space=SMEM)] + [pl.BlockSpec(memory_space=VMEM)] * (2 + len(shares)),
        out_specs=(pl.BlockSpec(memory_space=VMEM),) * (2 if closes else 1),
        scratch_shapes=[
            pltpu.VMEM((taps, share, outs), shares[0].dtype),
            pltpu.VMEM((images, rows, cols, share), features.dtype),
        ],
        input_output_aliases={} if opens else {2 + len(shares): 0},
        compiler_params=pltpu.CompilerParams(vmem_limit_bytes=VMEM_LIMIT),
    )(index, features, *shares, opening if opens else done)


def pick_kernel(*refs):
    *ins, out, sems = refs
    at, copies = 0, []
    for j, ref in enumerate(ins):
        copy = pltpu.make_async_copy(ref.at[1], out.at[pl.ds(at, ref.shape[1])], sems.at[j])
        copy.start()
        copies.append(copy)
        at += ref.shape[1]
    for copy in copies:
        copy.wait()


def middle_rows(kernels):
    _, taps, depth, outs = kernels[0].shape
    return pl.pallas_call(
        pick_kernel,
        out_shape=jax.ShapeDtypeStruct((taps * len(kernels), depth, outs), kernels[0].dtype),
        in_specs=[pl.BlockSpec(memory_space=pltpu.HBM)] * len(kernels),
        out_specs=pl.BlockSpec(memory_space=VMEM),
        scratch_shapes=[pltpu.SemaphoreType.DMA((len(kernels),))],
        compiler_params=pltpu.CompilerParams(vmem_limit_bytes=VMEM_LIMIT // 4),
        name="pick",
    )(*[pltpu.with_memory_space_constraint(kernel, pltpu.HBM) for kernel in kernels])


def project_kernel(groups, count, index_ref, pre_ref, total_ref, gain_ref, shift_ref, w_ref, pool_ref, proj_ref, stats_ref):
    images, rows, cols, width = pre_ref.shape
    outs = w_ref.shape[1]
    copies = stats_ref.shape[0]
    me = lax.axis_index("dp")
    gain = jnp.concatenate([gain_ref[pl.ds(k, 1), :] for k in range(gain_ref.shape[0])], 1)
    shift = jnp.concatenate([shift_ref[pl.ds(k, 1), :] for k in range(shift_ref.shape[0])], 1)

    def image(i, carry):
        group = index_ref[me * images + i]
        mean = pick_row(total_ref[pl.ds(0, groups), :], group) / count
        var = pick_row(total_ref[pl.ds(groups, groups), :], group) / count - mean * mean
        inv = lax.rsqrt(var + 1e-05)
        pre = pre_ref[i].reshape(rows * cols, width)
        scaled = (pre - mean) * inv * gain + shift
        branches = jnp.maximum(scaled, 0.0).astype(w_ref.dtype)
        proj = jnp.dot(branches, w_ref[pl.ds(0, width), :], preferred_element_type=jnp.float32)
        proj = proj + pool_ref[pl.ds(i, 1), :]
        proj_ref[i] = proj.reshape(rows, cols, outs)
        first = jnp.sum(proj, axis=0, keepdims=True)
        second = jnp.sum(proj * proj, axis=0, keepdims=True)
        stats_ref[:, pl.ds(2 * i, 1), :] = jnp.broadcast_to(first[None], (copies, 1, outs))
        stats_ref[:, pl.ds(2 * i + 1, 1), :] = jnp.broadcast_to(second[None], (copies, 1, outs))
        return carry

    for i in range(images):
        image(i, 0)


def finish_kernel(count, index_ref, proj_ref, sums_ref, gain_ref, shift_ref, out_ref):
    images, rows, cols, outs = proj_ref.shape
    places, planes = sums_ref.shape[:2]
    me = lax.axis_index("dp")
    each = []
    for p in range(places):
        both = sums_ref[p, 0]
        for r in range(1, planes):
            both = both + sums_ref[p, r]
        each.append(both)
    for i in range(images):
        group = index_ref[me * images + i]
        total = jnp.zeros((2, outs), jnp.float32)
        for p in range(places):
            for k in range(images):
                hit = index_ref[p * images + k] == group
                total = total + jnp.where(hit, each[p][2 * k : 2 * k + 2], 0.0)
        mean = total[0:1] / count
        var = total[1:2] / count - mean * mean
        inv = lax.rsqrt(var + 1e-05)
        proj = proj_ref[i].reshape(rows * cols, outs)
        scaled = (proj - mean) * inv * gain_ref[...] + shift_ref[...]
        out_ref[i] = jnp.maximum(scaled, 0.0).astype(out_ref.dtype).reshape(rows, cols, outs)


def finished(proj, sums, index, gain, shift, count):
    return pl.pallas_call(
        functools.partial(finish_kernel, count),
        out_shape=jax.ShapeDtypeStruct(proj.shape, jnp.bfloat16),
        in_specs=[pl.BlockSpec(memory_space=SMEM)] + [pl.BlockSpec(memory_space=VMEM)] * 4,
        out_specs=pl.BlockSpec(memory_space=VMEM),
        compiler_params=pltpu.CompilerParams(vmem_limit_bytes=VMEM_LIMIT),
        name="finish",
    )(index, proj, sums, gain, shift)


def normed_project(pre, totals, index, gain, shift, weight, pool_term, groups, count):
    images, rows, cols, _ = pre.shape
    outs = weight.shape[1]
    devices = lax.axis_size(("dp", "rows"))
    return pl.pallas_call(
        functools.partial(project_kernel, groups, count),
        out_shape=(
            jax.ShapeDtypeStruct((images, rows, cols, outs), jnp.float32),
            jax.ShapeDtypeStruct((devices, 2 * images, outs), jnp.float32),
        ),
        in_specs=[pl.BlockSpec(memory_space=SMEM)] + [pl.BlockSpec(memory_space=VMEM)] * 6,
        out_specs=(pl.BlockSpec(memory_space=VMEM),) * 2,
        compiler_params=pltpu.CompilerParams(vmem_limit_bytes=VMEM_LIMIT),
        name="project",
    )(index, pre, totals, gain, shift, weight, pool_term)


def far_swap(array, even, odd):
    count = lax.axis_size("rows")
    pairs = []
    for i in range(lax.axis_size("dp")):
        for j in range(count):
            k = i ^ (odd if j % 2 else even)
            pairs.append((i * count + j, k * count + j))
    return lax.ppermute(array, ("dp", "rows"), pairs)


def conv_branches(features, kernels, pointwise_weight, pool_term, index, groups):
    quarter = lax.axis_size("dp") // 4
    near = list(range(2, quarter, 2))
    one, two, three = quarter, 2 * quarter, 3 * quarter
    own = middle_rows(kernels)
    both, first, second = (one, one), (two, three), (three, two)

    def by(share, mask):
        return tuple(m ^ mask for m in share)

    origin = (0, 0)
    beside = [(m, m) for m in near]
    got, held = {origin: own}, {}

    def pass_on(mask):
        held[mask] = (got[mask], swap(got[mask], "dp", 1))

    got[first] = far_swap(own, *first)
    got[both] = swap(own, "dp", one)
    for mask in beside:
        got[mask] = swap(own, "dp", mask[0])
    pass_on(origin)
    for mask in beside:
        pass_on(mask)
    held[origin], pool_term = lax.optimization_barrier((held[origin], pool_term))
    opened = [origin] + beside
    (done,) = conv_part(features, held, opened, index, groups, pointwise_weight)
    for mask in near:
        got[by(first, mask)] = swap(got[first], "dp", mask)
    got[second] = swap(got[first], "rows", 1)
    for mask in near:
        got[by(both, mask)] = swap(got[both], "dp", mask)
    pass_on(first)
    pass_on(both)
    for mask in near:
        late = by(first, mask)
        got[late], done = lax.optimization_barrier((got[late], done))
        got[by(second, mask)] = swap(got[late], "rows", 1)
    pass_on(second)
    (done,) = conv_part(features, held, [first, both, second], index, groups, done=done)
    last = []
    for mask in near:
        pass_on(by(first, mask))
        late, final = by(both, mask), by(second, mask)
        got[late], done = lax.optimization_barrier((got[late], done))
        pass_on(late)
        pass_on(final)
        last += [by(first, mask), by(both, mask), final]
    pre, stats = conv_part(features, held, last, index, groups, done=done, closes=True)
    return pre, stats, pool_term


def row_tap_list(block_tensor, kernel_row_slice, dilation_rate):
    partial_terms = jnp.einsum(
        "irwc,kco->irwko", block_tensor, kernel_row_slice, preferred_element_type=jnp.float32
    )
    map_width = block_tensor.shape[2]
    left = jnp.pad(partial_terms[:, :, :, 0], ((0, 0), (0, 0), (dilation_rate, 0), (0, 0)))
    right = jnp.pad(partial_terms[:, :, :, 2], ((0, 0), (0, 0), (0, dilation_rate), (0, 0)))
    return partial_terms[:, :, :, 1] + left[:, :, :map_width] + right[:, :, dilation_rate:]


def general_pre(features, kernels, pointwise_weight):
    branches = [
        jnp.einsum("irwc,co->irwo", features, pointwise_weight, preferred_element_type=jnp.float32)
    ]
    for kernel, dilation in zip(kernels, DILATIONS):
        whole = lax.all_gather(kernel, "dp", axis=2, tiled=True)
        total = row_tap_list(features, whole[1], dilation)
        step = dilation // features.shape[1]
        if step < lax.axis_size("rows"):
            for by, tap in ((step, 0), (-step, 2)):
                total = total + from_behind(row_tap_list(features, whole[tap], dilation), "rows", by)
        branches.append(total)
    return jnp.concatenate(branches, -1)


def shards(
    features,
    first_atrous_weight,
    second_atrous_weight,
    third_atrous_weight,
    pointwise_weight,
    pooling_weight,
    projection_weight,
    branch_norm_gain,
    branch_norm_shift,
    projection_norm_gain,
    projection_norm_shift,
    ghost_group_index,
):
    images, rows_dev, cols, _ = features.shape
    dp_size = lax.axis_size("dp")
    rows_size = lax.axis_size("rows")
    groups = images * dp_size // 4
    pixels = rows_dev * rows_size * cols
    count = 4.0 * pixels
    width = branch_norm_gain.size
    own_groups = lax.dynamic_slice_in_dim(
        ghost_group_index, lax.axis_index("dp") * images, images, 0
    )
    kernels = (first_atrous_weight, second_atrous_weight, third_atrous_weight)
    pool_total = sum_over(jnp.sum(features, axis=(1, 2), dtype=jnp.float32), ("rows",))
    pooled = (pool_total / pixels).astype(jnp.bfloat16)
    pool_act = jax.nn.relu(
        jnp.dot(pooled, pooling_weight, preferred_element_type=jnp.float32)
    ).astype(jnp.bfloat16)
    pool_term = jnp.dot(pool_act, projection_weight[width:], preferred_element_type=jnp.float32)
    middle_only = all(d // rows_dev >= rows_size for d in DILATIONS)
    if middle_only and rows_size % 2 == 0 and dp_size >= 8 and dp_size & (dp_size - 1) == 0:
        pre, stats, pool_term = conv_branches(
            features, kernels, pointwise_weight, pool_term, ghost_group_index, groups
        )
    else:
        pre = general_pre(features, kernels, pointwise_weight)
        hot = (own_groups[:, None] == jnp.arange(groups, dtype=jnp.int32)[None, :]).astype(jnp.float32)
        stats = jnp.concatenate(
            [
                jnp.dot(hot.T, jnp.sum(t, axis=(1, 2)), precision=lax.Precision.HIGHEST)
                for t in (pre, pre * pre)
            ],
            0,
        )
    totals = sum_over(stats, ("dp", "rows"))
    proj, proj_stats = normed_project(
        pre,
        totals,
        ghost_group_index,
        branch_norm_gain,
        branch_norm_shift,
        projection_weight,
        pool_term,
        groups,
        count,
    )
    sums = lax.all_to_all(proj_stats, ("dp", "rows"), 0, 0, tiled=True)
    local_out = finished(
        proj,
        sums.reshape(dp_size, rows_size, 2 * images, -1),
        ghost_group_index,
        projection_norm_gain.reshape(1, -1),
        projection_norm_shift.reshape(1, -1),
        count,
    )
    return lax.all_to_all(local_out, "dp", split_axis=2, concat_axis=0, tiled=True)


def solution(mesh):
    in_specs = (
        P("dp", "rows", None, None),
        P(None, None, "dp", None),
        P(None, None, "dp", None),
        P(None, None, "dp", None),
        P(),
        P(),
        P(),
        P(),
        P(),
        P(),
        P(),
        P(),
    )
    out_specs = P(None, "rows", "dp", None)

    return jax.shard_map(shards, mesh=mesh, in_specs=in_specs, out_specs=out_specs, check_vma=False)
```

```python
import functools

import jax
import jax.numpy as jnp
from jax import lax
from jax.experimental import pallas as pl
from jax.experimental.pallas import tpu as pltpu
from jax.sharding import PartitionSpec as P

DILATIONS = (12, 24, 36)
VMEM = pltpu.VMEM
SMEM = pltpu.SMEM
VMEM_LIMIT = 26 * 2**20
WIDE = 2


def from_behind(array, axis, by):
    count = lax.axis_size(axis)
    pairs = [(i, i + by) for i in range(count) if 0 <= i + by < count]
    return lax.ppermute(array, axis, pairs)


def swap(array, axis, mask):
    return lax.ppermute(array, axis, [(i, i ^ mask) for i in range(lax.axis_size(axis))])


def masks_of(axis):
    size, mask, out = lax.axis_size(axis), 1, []
    while mask < size:
        out.append(mask)
        mask *= 2
    return out


def sum_over(array, axes):
    for axis in axes:
        size = lax.axis_size(axis)
        if size & (size - 1):
            array = lax.psum(array, axis)
            continue
        for mask in masks_of(axis):
            array = array + swap(array, axis, mask)
    return array


def peer(array, dp_mask, rows_mask):
    count = lax.axis_size("rows")
    size = lax.axis_size("dp") * count
    pairs = [(i, (i // count ^ dp_mask) * count + (i % count ^ rows_mask)) for i in range(size)]
    return lax.ppermute(array, ("dp", "rows"), pairs)


def total_over_all(stats):
    quarter = lax.axis_size("dp") // 4
    steps = [(mask, 0) for mask in masks_of("dp") if 1 < mask < quarter]
    steps += [(0, mask) for mask in masks_of("rows")]
    steps += [(quarter, 0), (2 * quarter, 0)]
    total = stats + swap(stats, "dp", 1)
    for i in range(0, len(steps), WIDE):
        moves = [(0, 0)]
        for a, b in steps[i : i + WIDE]:
            moves += [(a ^ c, b ^ d) for c, d in moves]
        total = sum((peer(total, *move) for move in moves[1:]), total)
    return total


def tap_span(cols, shift):
    low = max(0, -shift) // 16 * 16
    high = min(cols, -(-(cols - max(0, shift)) // 16) * 16)
    return low, high


def moved(part, low, cols, shift):
    rows, _, chans = part.shape
    if shift > 0:
        zeros = jnp.zeros((rows, shift, chans), part.dtype)
        return jnp.concatenate([zeros, part[:, : cols - shift]], axis=1)
    zeros = jnp.zeros((rows, -shift, chans), part.dtype)
    return jnp.concatenate([part[:, -shift - low :], zeros], axis=1)


def group_rows(groups, group, values):
    rows = lax.broadcasted_iota(jnp.int32, (groups, values.shape[-1]), 0)
    return jnp.where(rows == group, jnp.broadcast_to(values, rows.shape), 0.0)


def pick_row(table, group):
    rows = lax.broadcasted_iota(jnp.int32, table.shape, 0)
    return jnp.sum(jnp.where(rows == group, table, 0.0), axis=0, keepdims=True)


def conv_kernel(groups, masks, opens, closes, index_ref, x_ref, *rest):
    shares, rest = rest[: 2 * len(masks)], rest[2 * len(masks) :]
    if opens:
        pw_ref, pre_ref, *rest = rest
    else:
        done_ref, pre_ref, *rest = rest
    if closes:
        stats_ref, *rest = rest
        stats_ref[...] = jnp.zeros_like(stats_ref)
    w_ref, part_ref = rest
    images, _, cols, _ = x_ref.shape
    outs = w_ref.shape[2]
    depth = shares[0].shape[1]
    pair = 2 * depth
    me = lax.axis_index("dp")
    odd = lax.rem(lax.axis_index("rows"), 2)
    core = lax.rem(me, 2)
    here = pl.multiple_of(core * depth, depth)
    there = pl.multiple_of((1 - core) * depth, depth)
    for j, mask in enumerate(masks):
        w_ref[:, pl.ds(j * pair + here, depth), :] = shares[2 * j][...]
        w_ref[:, pl.ds(j * pair + there, depth), :] = shares[2 * j + 1][...]
        mask = mask[0] + odd * (mask[1] - mask[0])
        block = pl.multiple_of((me ^ mask) // 2 * pair, pair)
        part_ref[:, :, :, pl.ds(j * pair, pair)] = x_ref[:, :, :, pl.ds(block, pair)]

    def product(x, w):
        r, c, k = x.shape
        y = jnp.dot(x.reshape(r * c, k), w, preferred_element_type=jnp.float32)
        return y.reshape(r, c, outs)

    def image(i, carry):
        group = index_ref[me * images + i]

        def emit(branch, value):
            span = pl.ds(branch * outs, outs)
            if branch == 0 and not opens:
                value = done_ref[i, :, :, span]
            elif not opens:
                value = value + done_ref[i, :, :, span]
            pre_ref[i, :, :, span] = value
            if closes:
                first = jnp.sum(value, axis=(0, 1)).reshape(1, outs)
                second = jnp.sum(value * value, axis=(0, 1)).reshape(1, outs)
                stats_ref[pl.ds(0, groups), span] += group_rows(groups, group, first)
                stats_ref[pl.ds(groups, groups), span] += group_rows(groups, group, second)

        if opens:
            emit(0, product(x_ref[i], pw_ref[...]))
        elif closes:
            emit(0, None)
        for k, dilation in enumerate(DILATIONS):
            total = product(part_ref[i], w_ref[3 * k + 1])
            for tap, shift in ((0, dilation), (2, -dilation)):
                if abs(shift) < cols:
                    low, high = tap_span(cols, shift)
                    part = product(part_ref[i, :, pl.ds(low, high - low), :], w_ref[3 * k + tap])
                    total = total + moved(part, low, cols, shift)
            emit(k + 1, total)
        return carry

    lax.fori_loop(0, images, image, 0)


def conv_part(features, held, masks, index, groups, opening=None, done=None, closes=False):
    shares = [share for mask in masks for share in held[mask]]
    images, rows, cols, _ = features.shape
    taps, depth, outs = shares[0].shape
    share = 2 * depth * len(masks)
    width = outs * (1 + len(DILATIONS))
    pre = jax.ShapeDtypeStruct((images, rows, cols, width), jnp.float32)
    stats = jax.ShapeDtypeStruct((2 * groups, width), jnp.float32)
    opens = done is None
    return pl.pallas_call(
        functools.partial(conv_kernel, groups, tuple(masks), opens, closes),
        out_shape=(pre, stats) if closes else (pre,),
        in_specs=[pl.BlockSpec(memory_space=SMEM)] + [pl.BlockSpec(memory_space=VMEM)] * (2 + len(shares)),
        out_specs=(pl.BlockSpec(memory_space=VMEM),) * (2 if closes else 1),
        scratch_shapes=[
            pltpu.VMEM((taps, share, outs), shares[0].dtype),
            pltpu.VMEM((images, rows, cols, share), features.dtype),
        ],
        input_output_aliases={} if opens else {2 + len(shares): 0},
        compiler_params=pltpu.CompilerParams(vmem_limit_bytes=VMEM_LIMIT),
    )(index, features, *shares, opening if opens else done)


def pick_kernel(*refs):
    *ins, out, sems = refs
    at, copies = 0, []
    for j, ref in enumerate(ins):
        copy = pltpu.make_async_copy(ref.at[1], out.at[pl.ds(at, ref.shape[1])], sems.at[j])
        copy.start()
        copies.append(copy)
        at += ref.shape[1]
    for copy in copies:
        copy.wait()


def middle_rows(kernels):
    _, taps, depth, outs = kernels[0].shape
    return pl.pallas_call(
        pick_kernel,
        out_shape=jax.ShapeDtypeStruct((taps * len(kernels), depth, outs), kernels[0].dtype),
        in_specs=[pl.BlockSpec(memory_space=pltpu.HBM)] * len(kernels),
        out_specs=pl.BlockSpec(memory_space=VMEM),
        scratch_shapes=[pltpu.SemaphoreType.DMA((len(kernels),))],
        compiler_params=pltpu.CompilerParams(vmem_limit_bytes=VMEM_LIMIT // 4),
        name="pick",
    )(*[pltpu.with_memory_space_constraint(kernel, pltpu.HBM) for kernel in kernels])


def project_kernel(groups, count, index_ref, pre_ref, total_ref, gain_ref, shift_ref, w_ref, pool_ref, proj_ref, stats_ref):
    images, rows, cols, width = pre_ref.shape
    outs = w_ref.shape[1]
    copies = stats_ref.shape[0]
    me = lax.axis_index("dp")
    gain = jnp.concatenate([gain_ref[pl.ds(k, 1), :] for k in range(gain_ref.shape[0])], 1)
    shift = jnp.concatenate([shift_ref[pl.ds(k, 1), :] for k in range(shift_ref.shape[0])], 1)

    def image(i, carry):
        group = index_ref[me * images + i]
        mean = pick_row(total_ref[pl.ds(0, groups), :], group) / count
        var = pick_row(total_ref[pl.ds(groups, groups), :], group) / count - mean * mean
        inv = lax.rsqrt(var + 1e-05)
        pre = pre_ref[i].reshape(rows * cols, width)
        scaled = (pre - mean) * inv * gain + shift
        branches = jnp.maximum(scaled, 0.0).astype(w_ref.dtype)
        proj = jnp.dot(branches, w_ref[pl.ds(0, width), :], preferred_element_type=jnp.float32)
        proj = proj + pool_ref[pl.ds(i, 1), :]
        proj_ref[i] = proj.reshape(rows, cols, outs)
        first = jnp.sum(proj, axis=0, keepdims=True)
        second = jnp.sum(proj * proj, axis=0, keepdims=True)
        stats_ref[:, pl.ds(2 * i, 1), :] = jnp.broadcast_to(first[None], (copies, 1, outs))
        stats_ref[:, pl.ds(2 * i + 1, 1), :] = jnp.broadcast_to(second[None], (copies, 1, outs))
        return carry

    for i in range(images):
        image(i, 0)


def finish_kernel(count, index_ref, proj_ref, sums_ref, gain_ref, shift_ref, out_ref):
    images, rows, cols, outs = proj_ref.shape
    places, planes = sums_ref.shape[:2]
    me = lax.axis_index("dp")
    each = []
    for p in range(places):
        both = sums_ref[p, 0]
        for r in range(1, planes):
            both = both + sums_ref[p, r]
        each.append(both)
    for i in range(images):
        group = index_ref[me * images + i]
        total = jnp.zeros((2, outs), jnp.float32)
        for p in range(places):
            for k in range(images):
                hit = index_ref[p * images + k] == group
                total = total + jnp.where(hit, each[p][2 * k : 2 * k + 2], 0.0)
        mean = total[0:1] / count
        var = total[1:2] / count - mean * mean
        inv = lax.rsqrt(var + 1e-05)
        proj = proj_ref[i].reshape(rows * cols, outs)
        scaled = (proj - mean) * inv * gain_ref[...] + shift_ref[...]
        tiles, wide = out_ref.shape[0], out_ref.shape[3]
        result = jnp.maximum(scaled, 0.0).reshape(rows, tiles, wide, outs)
        for h in range(rows):
            out_ref[:, i, h] = result[h].astype(out_ref.dtype)


def finished(proj, sums, index, gain, shift, count):
    images, rows, cols, outs = proj.shape
    tiles = lax.axis_size("dp")
    return pl.pallas_call(
        functools.partial(finish_kernel, count),
        out_shape=jax.ShapeDtypeStruct((tiles, images, rows, cols // tiles, outs), jnp.bfloat16),
        in_specs=[pl.BlockSpec(memory_space=SMEM)] + [pl.BlockSpec(memory_space=VMEM)] * 4,
        out_specs=pl.BlockSpec(memory_space=VMEM),
        compiler_params=pltpu.CompilerParams(vmem_limit_bytes=VMEM_LIMIT),
        name="finish",
    )(index, proj, sums, gain, shift)


def normed_project(pre, totals, index, gain, shift, weight, pool_term, groups, count):
    images, rows, cols, _ = pre.shape
    outs = weight.shape[1]
    devices = lax.axis_size(("dp", "rows"))
    return pl.pallas_call(
        functools.partial(project_kernel, groups, count),
        out_shape=(
            jax.ShapeDtypeStruct((images, rows, cols, outs), jnp.float32),
            jax.ShapeDtypeStruct((devices, 2 * images, outs), jnp.float32),
        ),
        in_specs=[pl.BlockSpec(memory_space=SMEM)] + [pl.BlockSpec(memory_space=VMEM)] * 6,
        out_specs=(pl.BlockSpec(memory_space=VMEM),) * 2,
        compiler_params=pltpu.CompilerParams(vmem_limit_bytes=VMEM_LIMIT),
        name="project",
    )(index, pre, totals, gain, shift, weight, pool_term)


def far_swap(array, even, odd):
    count = lax.axis_size("rows")
    pairs = []
    for i in range(lax.axis_size("dp")):
        for j in range(count):
            k = i ^ (odd if j % 2 else even)
            pairs.append((i * count + j, k * count + j))
    return lax.ppermute(array, ("dp", "rows"), pairs)


def conv_branches(features, kernels, pointwise_weight, pool_term, index, groups):
    quarter = lax.axis_size("dp") // 4
    near = list(range(2, quarter, 2))
    one, two, three = quarter, 2 * quarter, 3 * quarter
    own = middle_rows(kernels)
    both, first, second = (one, one), (two, three), (three, two)

    def by(share, mask):
        return tuple(m ^ mask for m in share)

    origin = (0, 0)
    beside = [(m, m) for m in near]
    got, held = {origin: own}, {}

    def pass_on(mask):
        held[mask] = (got[mask], swap(got[mask], "dp", 1))

    got[first] = far_swap(own, *first)
    got[both] = swap(own, "dp", one)
    for mask in beside:
        got[mask] = swap(own, "dp", mask[0])
    pass_on(origin)
    for mask in beside:
        pass_on(mask)
    got[first], pool_term = lax.optimization_barrier((got[first], pool_term))
    for mask in near:
        got[by(first, mask)] = swap(got[first], "dp", mask)
    got[second] = swap(got[first], "rows", 1)
    for mask in near:
        got[by(both, mask)] = swap(got[both], "dp", mask)
    pass_on(both)
    pass_on(first)
    opened = [origin, both, first] + beside
    (done,) = conv_part(features, held, opened, index, groups, pointwise_weight)
    relayed = []
    for mask in near:
        late = by(first, mask)
        got[late], done = lax.optimization_barrier((got[late], done))
        got[by(second, mask)] = swap(got[late], "rows", 1)
        pass_on(late)
        relayed.append(late)
    pass_on(second)
    (done,) = conv_part(features, held, [second] + relayed, index, groups, done=done)
    last = []
    for mask in near:
        late, final = by(both, mask), by(second, mask)
        got[late], done = lax.optimization_barrier((got[late], done))
        pass_on(late)
        pass_on(final)
        last += [late, final]
    pre, stats = conv_part(features, held, last, index, groups, done=done, closes=True)
    return pre, total_over_all(stats), pool_term


def row_tap_list(block_tensor, kernel_row_slice, dilation_rate):
    partial_terms = jnp.einsum(
        "irwc,kco->irwko", block_tensor, kernel_row_slice, preferred_element_type=jnp.float32
    )
    map_width = block_tensor.shape[2]
    left = jnp.pad(partial_terms[:, :, :, 0], ((0, 0), (0, 0), (dilation_rate, 0), (0, 0)))
    right = jnp.pad(partial_terms[:, :, :, 2], ((0, 0), (0, 0), (0, dilation_rate), (0, 0)))
    return partial_terms[:, :, :, 1] + left[:, :, :map_width] + right[:, :, dilation_rate:]


def general_pre(features, kernels, pointwise_weight):
    branches = [
        jnp.einsum("irwc,co->irwo", features, pointwise_weight, preferred_element_type=jnp.float32)
    ]
    for kernel, dilation in zip(kernels, DILATIONS):
        whole = lax.all_gather(kernel, "dp", axis=2, tiled=True)
        total = row_tap_list(features, whole[1], dilation)
        step = dilation // features.shape[1]
        if step < lax.axis_size("rows"):
            for by, tap in ((step, 0), (-step, 2)):
                total = total + from_behind(row_tap_list(features, whole[tap], dilation), "rows", by)
        branches.append(total)
    return jnp.concatenate(branches, -1)


def shards(
    features,
    first_atrous_weight,
    second_atrous_weight,
    third_atrous_weight,
    pointwise_weight,
    pooling_weight,
    projection_weight,
    branch_norm_gain,
    branch_norm_shift,
    projection_norm_gain,
    projection_norm_shift,
    ghost_group_index,
):
    images, rows_dev, cols, _ = features.shape
    dp_size = lax.axis_size("dp")
    rows_size = lax.axis_size("rows")
    groups = images * dp_size // 4
    pixels = rows_dev * rows_size * cols
    count = 4.0 * pixels
    width = branch_norm_gain.size
    own_groups = lax.dynamic_slice_in_dim(
        ghost_group_index, lax.axis_index("dp") * images, images, 0
    )
    kernels = (first_atrous_weight, second_atrous_weight, third_atrous_weight)
    pool_total = sum_over(jnp.sum(features, axis=(1, 2), dtype=jnp.float32), ("rows",))
    pooled = (pool_total / pixels).astype(jnp.bfloat16)
    pool_act = jax.nn.relu(
        jnp.dot(pooled, pooling_weight, preferred_element_type=jnp.float32)
    ).astype(jnp.bfloat16)
    pool_term = jnp.dot(pool_act, projection_weight[width:], preferred_element_type=jnp.float32)
    middle_only = all(d // rows_dev >= rows_size for d in DILATIONS)
    if middle_only and rows_size % 2 == 0 and dp_size >= 8 and dp_size & (dp_size - 1) == 0:
        pre, totals, pool_term = conv_branches(
            features, kernels, pointwise_weight, pool_term, ghost_group_index, groups
        )
    else:
        pre = general_pre(features, kernels, pointwise_weight)
        hot = (own_groups[:, None] == jnp.arange(groups, dtype=jnp.int32)[None, :]).astype(jnp.float32)
        stats = jnp.concatenate(
            [
                jnp.dot(hot.T, jnp.sum(t, axis=(1, 2)), precision=lax.Precision.HIGHEST)
                for t in (pre, pre * pre)
            ],
            0,
        )
        totals = sum_over(stats, ("dp", "rows"))
    proj, proj_stats = normed_project(
        pre,
        totals,
        ghost_group_index,
        branch_norm_gain,
        branch_norm_shift,
        projection_weight,
        pool_term,
        groups,
        count,
    )
    sums = lax.all_to_all(proj_stats, ("dp", "rows"), 0, 0, tiled=True)
    local_out = finished(
        proj,
        sums.reshape(dp_size, rows_size, 2 * images, -1),
        ghost_group_index,
        projection_norm_gain.reshape(1, -1),
        projection_norm_shift.reshape(1, -1),
        count,
    )
    local_out = local_out.reshape(dp_size * images, *local_out.shape[2:])
    return lax.all_to_all(local_out, "dp", 0, 0, tiled=True)


def solution(mesh):
    in_specs = (
        P("dp", "rows", None, None),
        P(None, None, "dp", None),
        P(None, None, "dp", None),
        P(None, None, "dp", None),
        P(),
        P(),
        P(),
        P(),
        P(),
        P(),
        P(),
        P(),
    )
    out_specs = P(None, "rows", "dp", None)

    return jax.shard_map(shards, mesh=mesh, in_specs=in_specs, out_specs=out_specs, check_vma=False)
```

```python
import functools

import jax
import jax.numpy as jnp
from jax import lax
from jax.experimental import pallas as pl
from jax.experimental.pallas import tpu as pltpu
from jax.sharding import PartitionSpec as P

DILATIONS = (12, 24, 36)
VMEM = pltpu.VMEM
SMEM = pltpu.SMEM
VMEM_LIMIT = 26 * 2**20


def from_behind(array, axis, by):
    count = lax.axis_size(axis)
    pairs = [(i, i + by) for i in range(count) if 0 <= i + by < count]
    return lax.ppermute(array, axis, pairs)


def swap(array, axis, mask):
    return lax.ppermute(array, axis, [(i, i ^ mask) for i in range(lax.axis_size(axis))])


def masks_of(axis):
    size, mask, out = lax.axis_size(axis), 1, []
    while mask < size:
        out.append(mask)
        mask *= 2
    return out


def sum_over(array, axes):
    for axis in axes:
        size = lax.axis_size(axis)
        if size & (size - 1):
            array = lax.psum(array, axis)
            continue
        for mask in masks_of(axis):
            array = array + swap(array, axis, mask)
    return array


def regroup_kernel(planes, index_ref, sums_ref, out_ref):
    places, both, _ = sums_ref.shape
    images = both // 2
    groups = out_ref.shape[0] // 2
    lines = places // planes
    base = lax.axis_index("dp") // lines * lines * images
    out_ref[...] = jnp.zeros_like(out_ref)
    for p in range(lines):
        for i in range(images):
            group = index_ref[base + p * images + i]
            for part in range(2):
                row = sums_ref[p * planes, pl.ds(part * images + i, 1), :]
                for r in range(1, planes):
                    row = row + sums_ref[p * planes + r, pl.ds(part * images + i, 1), :]
                span = pl.ds(part * groups, groups)
                out_ref[span, :] += group_rows(groups, group, row)


def total_over_all(sums, index, groups):
    slab, _, width = sums.shape
    size = lax.axis_size(("dp", "rows"))
    teams = [list(range(i, i + slab)) for i in range(0, size, slab)]
    sums = lax.all_to_all(sums, ("dp", "rows"), 0, 0, tiled=True, axis_index_groups=teams)
    total = pl.pallas_call(
        functools.partial(regroup_kernel, lax.axis_size("rows")),
        out_shape=jax.ShapeDtypeStruct((2 * groups, width), jnp.float32),
        in_specs=[pl.BlockSpec(memory_space=SMEM), pl.BlockSpec(memory_space=VMEM)],
        out_specs=pl.BlockSpec(memory_space=VMEM),
        compiler_params=pltpu.CompilerParams(vmem_limit_bytes=VMEM_LIMIT),
        name="regroup",
    )(index, sums)
    quarter = lax.axis_size("dp") // 4
    total = sum((swap(total, "dp", quarter * j) for j in (1, 2, 3)), total)
    return total, swap(total, "dp", 1)


def tap_span(cols, shift):
    low = max(0, -shift) // 16 * 16
    high = min(cols, -(-(cols - max(0, shift)) // 16) * 16)
    return low, high


def moved(part, low, cols, shift):
    rows, _, chans = part.shape
    if shift > 0:
        zeros = jnp.zeros((rows, shift, chans), part.dtype)
        return jnp.concatenate([zeros, part[:, : cols - shift]], axis=1)
    zeros = jnp.zeros((rows, -shift, chans), part.dtype)
    return jnp.concatenate([part[:, -shift - low :], zeros], axis=1)


def group_rows(groups, group, values):
    rows = lax.broadcasted_iota(jnp.int32, (groups, values.shape[-1]), 0)
    return jnp.where(rows == group, jnp.broadcast_to(values, rows.shape), 0.0)


def pick_row(table, group):
    rows = lax.broadcasted_iota(jnp.int32, table.shape, 0)
    return jnp.sum(jnp.where(rows == group, table, 0.0), axis=0, keepdims=True)


def conv_kernel(planes, masks, opens, closes, index_ref, x_ref, *rest):
    shares, rest = rest[: 2 * len(masks)], rest[2 * len(masks) :]
    if opens:
        pw_ref, pre_ref, *rest = rest
    else:
        done_ref, pre_ref, *rest = rest
    if closes:
        stats_ref, *rest = rest
        copies = stats_ref.shape[0]
    w_ref, part_ref = rest
    images, _, cols, _ = x_ref.shape
    outs = w_ref.shape[2]
    depth = shares[0].shape[1]
    pair = 2 * depth
    me = lax.axis_index("dp")
    odd = lax.rem(lax.axis_index("rows"), 2)
    core = lax.rem(me, 2)
    here = pl.multiple_of(core * depth, depth)
    there = pl.multiple_of((1 - core) * depth, depth)
    for j, mask in enumerate(masks):
        w_ref[:, pl.ds(j * pair + here, depth), :] = shares[2 * j][...]
        w_ref[:, pl.ds(j * pair + there, depth), :] = shares[2 * j + 1][...]
        mask = mask[0] + odd * (mask[1] - mask[0])
        block = pl.multiple_of((me ^ mask) // 2 * pair, pair)
        part_ref[:, :, :, pl.ds(j * pair, pair)] = x_ref[:, :, :, pl.ds(block, pair)]

    def product(x, w):
        r, c, k = x.shape
        y = jnp.dot(x.reshape(r * c, k), w, preferred_element_type=jnp.float32)
        return y.reshape(r, c, outs)

    def image(i, carry):
        def emit(branch, value):
            span = pl.ds(branch * outs, outs)
            if branch == 0 and not opens:
                value = done_ref[i, :, :, span]
            elif not opens:
                value = value + done_ref[i, :, :, span]
            if opens or branch:
                pre_ref[i, :, :, span] = value
            if closes:
                first = jnp.sum(value, axis=(0, 1)).reshape(1, outs)
                second = jnp.sum(value * value, axis=(0, 1)).reshape(1, outs)
                wide = stats_ref.shape[2]
                half, at = divmod(branch * outs, wide)
                span = pl.ds(at, outs)
                for j in range(copies):
                    if j // planes % 2 == half:
                        stats_ref[j, pl.ds(i, 1), span] = first
                        stats_ref[j, pl.ds(images + i, 1), span] = second

        if opens:
            emit(0, product(x_ref[i], pw_ref[...]))
        elif closes:
            emit(0, None)
        for k, dilation in enumerate(DILATIONS):
            total = product(part_ref[i], w_ref[3 * k + 1])
            for tap, shift in ((0, dilation), (2, -dilation)):
                if abs(shift) < cols:
                    low, high = tap_span(cols, shift)
                    part = product(part_ref[i, :, pl.ds(low, high - low), :], w_ref[3 * k + tap])
                    total = total + moved(part, low, cols, shift)
            emit(k + 1, total)
        return carry

    lax.fori_loop(0, images, image, 0)


def conv_part(features, held, masks, index, opening=None, done=None, closes=False):
    shares = [share for mask in masks for share in held[mask]]
    images, rows, cols, _ = features.shape
    taps, depth, outs = shares[0].shape
    share = 2 * depth * len(masks)
    width = outs * (1 + len(DILATIONS))
    pre = jax.ShapeDtypeStruct((images, rows, cols, width), jnp.float32)
    slab = lax.axis_size("dp") // 4 * lax.axis_size("rows")
    stats = jax.ShapeDtypeStruct((slab, 2 * images, width // 2), jnp.float32)
    opens = done is None
    return pl.pallas_call(
        functools.partial(conv_kernel, lax.axis_size("rows"), tuple(masks), opens, closes),
        out_shape=(pre, stats) if closes else (pre,),
        in_specs=[pl.BlockSpec(memory_space=SMEM)] + [pl.BlockSpec(memory_space=VMEM)] * (2 + len(shares)),
        out_specs=(pl.BlockSpec(memory_space=VMEM),) * (2 if closes else 1),
        scratch_shapes=[
            pltpu.VMEM((taps, share, outs), shares[0].dtype),
            pltpu.VMEM((images, rows, cols, share), features.dtype),
        ],
        input_output_aliases={} if opens else {2 + len(shares): 0},
        compiler_params=pltpu.CompilerParams(vmem_limit_bytes=VMEM_LIMIT),
    )(index, features, *shares, opening if opens else done)


def pick_kernel(*refs):
    *ins, out, sems = refs
    at, copies = 0, []
    for j, ref in enumerate(ins):
        copy = pltpu.make_async_copy(ref.at[1], out.at[pl.ds(at, ref.shape[1])], sems.at[j])
        copy.start()
        copies.append(copy)
        at += ref.shape[1]
    for copy in copies:
        copy.wait()


def middle_rows(kernels):
    _, taps, depth, outs = kernels[0].shape
    return pl.pallas_call(
        pick_kernel,
        out_shape=jax.ShapeDtypeStruct((taps * len(kernels), depth, outs), kernels[0].dtype),
        in_specs=[pl.BlockSpec(memory_space=pltpu.HBM)] * len(kernels),
        out_specs=pl.BlockSpec(memory_space=VMEM),
        scratch_shapes=[pltpu.SemaphoreType.DMA((len(kernels),))],
        compiler_params=pltpu.CompilerParams(vmem_limit_bytes=VMEM_LIMIT // 4),
        name="pick",
    )(*[pltpu.with_memory_space_constraint(kernel, pltpu.HBM) for kernel in kernels])


def project_kernel(groups, count, index_ref, pre_ref, mine_ref, other_ref, gain_ref, shift_ref, w_ref, pool_ref, proj_ref, stats_ref):
    images, rows, cols, width = pre_ref.shape
    outs = w_ref.shape[1]
    copies = stats_ref.shape[0]
    me = lax.axis_index("dp")
    gain = jnp.concatenate([gain_ref[pl.ds(k, 1), :] for k in range(gain_ref.shape[0])], 1)
    shift = jnp.concatenate([shift_ref[pl.ds(k, 1), :] for k in range(shift_ref.shape[0])], 1)

    def image(i, carry):
        group = index_ref[me * images + i]

        def total(at):
            mine = pick_row(mine_ref[pl.ds(at, groups), :], group)
            other = pick_row(other_ref[pl.ds(at, groups), :], group)
            low_here = lax.rem(me, 2) == 0
            low, high = jnp.where(low_here, mine, other), jnp.where(low_here, other, mine)
            return jnp.concatenate([low, high], 1)

        mean = total(0) / count
        var = total(groups) / count - mean * mean
        inv = lax.rsqrt(var + 1e-05)
        pre = pre_ref[i].reshape(rows * cols, width)
        scaled = (pre - mean) * inv * gain + shift
        branches = jnp.maximum(scaled, 0.0).astype(w_ref.dtype)
        proj = jnp.dot(branches, w_ref[pl.ds(0, width), :], preferred_element_type=jnp.float32)
        proj = proj + pool_ref[pl.ds(i, 1), :]
        proj_ref[i] = proj.reshape(rows, cols, outs)
        first = jnp.sum(proj, axis=0, keepdims=True)
        second = jnp.sum(proj * proj, axis=0, keepdims=True)
        stats_ref[:, pl.ds(2 * i, 1), :] = jnp.broadcast_to(first[None], (copies, 1, outs))
        stats_ref[:, pl.ds(2 * i + 1, 1), :] = jnp.broadcast_to(second[None], (copies, 1, outs))
        return carry

    for i in range(images):
        image(i, 0)


def finish_kernel(count, index_ref, proj_ref, sums_ref, gain_ref, shift_ref, out_ref):
    images, rows, cols, outs = proj_ref.shape
    places, planes = sums_ref.shape[:2]
    me = lax.axis_index("dp")
    each = []
    for p in range(places):
        both = sums_ref[p, 0]
        for r in range(1, planes):
            both = both + sums_ref[p, r]
        each.append(both)
    for i in range(images):
        group = index_ref[me * images + i]
        total = jnp.zeros((2, outs), jnp.float32)
        for p in range(places):
            for k in range(images):
                hit = index_ref[p * images + k] == group
                total = total + jnp.where(hit, each[p][2 * k : 2 * k + 2], 0.0)
        mean = total[0:1] / count
        var = total[1:2] / count - mean * mean
        inv = lax.rsqrt(var + 1e-05)
        proj = proj_ref[i].reshape(rows * cols, outs)
        scaled = (proj - mean) * inv * gain_ref[...] + shift_ref[...]
        tiles, wide = out_ref.shape[0], out_ref.shape[3]
        result = jnp.maximum(scaled, 0.0).reshape(rows, tiles, wide, outs)
        for h in range(rows):
            out_ref[:, i, h] = result[h].astype(out_ref.dtype)


def finished(proj, sums, index, gain, shift, count):
    images, rows, cols, outs = proj.shape
    tiles = lax.axis_size("dp")
    return pl.pallas_call(
        functools.partial(finish_kernel, count),
        out_shape=jax.ShapeDtypeStruct((tiles, images, rows, cols // tiles, outs), jnp.bfloat16),
        in_specs=[pl.BlockSpec(memory_space=SMEM)] + [pl.BlockSpec(memory_space=VMEM)] * 4,
        out_specs=pl.BlockSpec(memory_space=VMEM),
        compiler_params=pltpu.CompilerParams(vmem_limit_bytes=VMEM_LIMIT),
        name="finish",
    )(index, proj, sums, gain, shift)


def normed_project(pre, totals, index, gain, shift, weight, pool_term, groups, count):
    images, rows, cols, _ = pre.shape
    outs = weight.shape[1]
    devices = lax.axis_size(("dp", "rows"))
    return pl.pallas_call(
        functools.partial(project_kernel, groups, count),
        out_shape=(
            jax.ShapeDtypeStruct((images, rows, cols, outs), jnp.float32),
            jax.ShapeDtypeStruct((devices, 2 * images, outs), jnp.float32),
        ),
        in_specs=[pl.BlockSpec(memory_space=SMEM)] + [pl.BlockSpec(memory_space=VMEM)] * 7,
        out_specs=(pl.BlockSpec(memory_space=VMEM),) * 2,
        compiler_params=pltpu.CompilerParams(vmem_limit_bytes=VMEM_LIMIT),
        name="project",
    )(index, pre, *totals, gain, shift, weight, pool_term)


def far_swap(array, even, odd):
    count = lax.axis_size("rows")
    pairs = []
    for i in range(lax.axis_size("dp")):
        for j in range(count):
            k = i ^ (odd if j % 2 else even)
            pairs.append((i * count + j, k * count + j))
    return lax.ppermute(array, ("dp", "rows"), pairs)


def conv_branches(features, kernels, pointwise_weight, pool_term, index, groups):
    quarter = lax.axis_size("dp") // 4
    near = list(range(2, quarter, 2))
    one, two, three = quarter, 2 * quarter, 3 * quarter
    own = middle_rows(kernels)
    both, first, second = (one, one), (two, three), (three, two)

    def by(share, mask):
        return tuple(m ^ mask for m in share)

    origin = (0, 0)
    beside = [(m, m) for m in near]
    got, held = {origin: own}, {}

    def pass_on(mask):
        held[mask] = (got[mask], swap(got[mask], "dp", 1))

    got[first] = far_swap(own, *first)
    got[both] = swap(own, "dp", one)
    for mask in beside:
        got[mask] = swap(own, "dp", mask[0])
    pass_on(origin)
    for mask in beside:
        pass_on(mask)
    got[first], pool_term = lax.optimization_barrier((got[first], pool_term))
    for mask in near:
        got[by(first, mask)] = swap(got[first], "dp", mask)
    got[second] = swap(got[first], "rows", 1)
    pass_on(both)
    pass_on(first)
    opened = [origin, both, first] + beside
    (done,) = conv_part(features, held, opened, index, pointwise_weight)
    got[both], done = lax.optimization_barrier((got[both], done))
    for mask in near:
        got[by(both, mask)] = swap(got[both], "dp", mask)
    relayed = []
    for mask in near:
        late = by(first, mask)
        got[late], done = lax.optimization_barrier((got[late], done))
        got[by(second, mask)] = swap(got[late], "rows", 1)
        pass_on(late)
        relayed.append(late)
    pass_on(second)
    (done,) = conv_part(features, held, [second] + relayed, index, done=done)
    last = []
    for mask in near:
        late, final = by(both, mask), by(second, mask)
        got[late], done = lax.optimization_barrier((got[late], done))
        pass_on(late)
        pass_on(final)
        last += [late, final]
    pre, stats = conv_part(features, held, last, index, done=done, closes=True)
    return pre, total_over_all(stats, index, groups), pool_term


def row_tap_list(block_tensor, kernel_row_slice, dilation_rate):
    partial_terms = jnp.einsum(
        "irwc,kco->irwko", block_tensor, kernel_row_slice, preferred_element_type=jnp.float32
    )
    map_width = block_tensor.shape[2]
    left = jnp.pad(partial_terms[:, :, :, 0], ((0, 0), (0, 0), (dilation_rate, 0), (0, 0)))
    right = jnp.pad(partial_terms[:, :, :, 2], ((0, 0), (0, 0), (0, dilation_rate), (0, 0)))
    return partial_terms[:, :, :, 1] + left[:, :, :map_width] + right[:, :, dilation_rate:]


def general_pre(features, kernels, pointwise_weight):
    branches = [
        jnp.einsum("irwc,co->irwo", features, pointwise_weight, preferred_element_type=jnp.float32)
    ]
    for kernel, dilation in zip(kernels, DILATIONS):
        whole = lax.all_gather(kernel, "dp", axis=2, tiled=True)
        total = row_tap_list(features, whole[1], dilation)
        step = dilation // features.shape[1]
        if step < lax.axis_size("rows"):
            for by, tap in ((step, 0), (-step, 2)):
                total = total + from_behind(row_tap_list(features, whole[tap], dilation), "rows", by)
        branches.append(total)
    return jnp.concatenate(branches, -1)


def shards(
    features,
    first_atrous_weight,
    second_atrous_weight,
    third_atrous_weight,
    pointwise_weight,
    pooling_weight,
    projection_weight,
    branch_norm_gain,
    branch_norm_shift,
    projection_norm_gain,
    projection_norm_shift,
    ghost_group_index,
):
    images, rows_dev, cols, _ = features.shape
    dp_size = lax.axis_size("dp")
    rows_size = lax.axis_size("rows")
    groups = images * dp_size // 4
    pixels = rows_dev * rows_size * cols
    count = 4.0 * pixels
    width = branch_norm_gain.size
    own_groups = lax.dynamic_slice_in_dim(
        ghost_group_index, lax.axis_index("dp") * images, images, 0
    )
    kernels = (first_atrous_weight, second_atrous_weight, third_atrous_weight)
    pool_total = sum_over(jnp.sum(features, axis=(1, 2), dtype=jnp.float32), ("rows",))
    pooled = (pool_total / pixels).astype(jnp.bfloat16)
    pool_act = jax.nn.relu(
        jnp.dot(pooled, pooling_weight, preferred_element_type=jnp.float32)
    ).astype(jnp.bfloat16)
    pool_term = jnp.dot(pool_act, projection_weight[width:], preferred_element_type=jnp.float32)
    middle_only = all(d // rows_dev >= rows_size for d in DILATIONS)
    if middle_only and rows_size % 2 == 0 and dp_size >= 8 and dp_size & (dp_size - 1) == 0:
        pre, totals, pool_term = conv_branches(
            features, kernels, pointwise_weight, pool_term, ghost_group_index, groups
        )
    else:
        pre = general_pre(features, kernels, pointwise_weight)
        hot = (own_groups[:, None] == jnp.arange(groups, dtype=jnp.int32)[None, :]).astype(jnp.float32)
        stats = jnp.concatenate(
            [
                jnp.dot(hot.T, jnp.sum(t, axis=(1, 2)), precision=lax.Precision.HIGHEST)
                for t in (pre, pre * pre)
            ],
            0,
        )
        low, high = jnp.split(sum_over(stats, ("dp", "rows")), 2, axis=1)
        core = lax.axis_index("dp") % 2
        totals = jnp.where(core == 0, low, high), jnp.where(core == 0, high, low)
    proj, proj_stats = normed_project(
        pre,
        totals,
        ghost_group_index,
        branch_norm_gain,
        branch_norm_shift,
        projection_weight,
        pool_term,
        groups,
        count,
    )
    sums = lax.all_to_all(proj_stats, ("dp", "rows"), 0, 0, tiled=True)
    local_out = finished(
        proj,
        sums.reshape(dp_size, rows_size, 2 * images, -1),
        ghost_group_index,
        projection_norm_gain.reshape(1, -1),
        projection_norm_shift.reshape(1, -1),
        count,
    )
    local_out = local_out.reshape(dp_size * images, *local_out.shape[2:])
    return lax.all_to_all(local_out, "dp", 0, 0, tiled=True)


def solution(mesh):
    in_specs = (
        P("dp", "rows", None, None),
        P(None, None, "dp", None),
        P(None, None, "dp", None),
        P(None, None, "dp", None),
        P(),
        P(),
        P(),
        P(),
        P(),
        P(),
        P(),
        P(),
    )
    out_specs = P(None, "rows", "dp", None)

    return jax.shard_map(shards, mesh=mesh, in_specs=in_specs, out_specs=out_specs, check_vma=False)
```
